32 devices in a mesh: atoms: 32 (over z, y, x, core).
Axes of the slice: x: 2, y: 2, z: 4, core: 2. Of those that a mesh axis runs over, the one named last changes fastest.
Arguments:
- features: bfloat16 [4096, 9, 128], P('atoms'), may hold values from -6 to 6
- cotangent: bfloat16 [4096, 9, 128], P('atoms'), may hold values from -6 to 6
- wigner: float32 [9, 9, 12288], P(None, None, 'atoms'), may hold values from -1 to 1, as said below
- pair_blocks: int32 [512, 2], P('atoms'), may hold values from 0 to 31, all different within a row; in each aligned block of 16 rows (0 to 15, 16 to 31, ...) at most 2 rows name the same one
- pair_rows: int32 [2, 6, 512], P(None, None, 'atoms'), may hold values from 0 to 127
- edge_ends: int32 [2, 12288], P(None, 'atoms'), may hold values from 0 to 5
- first_m0: bfloat16 [768, 512], replicated, may hold values from -0.21875 to 0.21875
- first_m1: bfloat16 [2, 512, 256], replicated, may hold values from -0.1875 to 0.1875
- first_m2: bfloat16 [2, 256, 128], replicated, may hold values from -0.25 to 0.25
- second_m0: bfloat16 [384, 384], replicated, may hold values from -0.3125 to 0.3125
- second_m1: bfloat16 [2, 256, 256], replicated, may hold values from -0.25 to 0.25
- second_m2: bfloat16 [2, 128, 128], replicated, may hold values from -0.375 to 0.375
Outputs:
- messages: bfloat16 [4096, 9, 128], P('atoms')
- grad_features: float32 [4096, 9, 128], P('atoms')
- grad_first_m0: float32 [768, 512], replicated
- grad_first_m1: float32 [2, 512, 256], replicated
- grad_first_m2: float32 [2, 256, 128], replicated
- grad_second_m0: float32 [384, 384], replicated
- grad_second_m1: float32 [2, 256, 256], replicated
- grad_second_m2: float32 [2, 128, 128], replicated
The draws below stay inside these ranges and needn't reach their ends.
Inputs may be any that keep to these rules, and one draw needn't show every extreme that they name: `pair_blocks`: among the 16 pairs of one device no atom block is named more than 2 times; the two blocks of a pair differ. `wigner`: each edge's matrix is orthogonal and block diagonal over degrees 0, 1 and 2.
All inputs are finite; a program needn't handle non-finite values.
Results may differ from the reference program's by a relative error of at most 0.0045.
Values may be sent and summed in bfloat16 or wider, within the bound.
A program may use at most 128 MiB of HBM per device.

```python
import math
import jax
import jax.numpy as jnp
import numpy as np
from jax import lax

C = 128
COEF = 9
BLK = 128
RPP = 6
EPP = 24
PAIRS_DEV = 16
MOST = 2
ATOMS = 4096
PAIRS = 512
EDGES = 12288
N_ATOMS = 32


def quad_table():
    table = np.zeros((5, 3, 3), dtype=np.float32)
    root_half = 1.0 / np.sqrt(2.0)
    table[0, 0, 1] = root_half
    table[0, 1, 0] = root_half
    table[1, 1, 2] = root_half
    table[1, 2, 1] = root_half
    table[2, 0, 0] = -1.0 / np.sqrt(6.0)
    table[2, 1, 1] = -1.0 / np.sqrt(6.0)
    table[2, 2, 2] = 2.0 / np.sqrt(6.0)
    table[3, 0, 2] = root_half
    table[3, 2, 0] = root_half
    table[4, 0, 0] = root_half
    table[4, 1, 1] = -root_half
    return table


def draw_wigner(key, part):
    quaternion = jax.random.normal(key, (4, EDGES), jnp.float32)
    quaternion = quaternion / jnp.sqrt(jnp.sum(quaternion * quaternion, axis=0, keepdims=True) + 1e-12)
    qw = quaternion[0]
    qx = quaternion[1]
    qy = quaternion[2]
    qz = quaternion[3]
    rotation = jnp.stack([jnp.stack([1.0 - 2.0 * (qy * qy + qz * qz), 2.0 * (qx * qy - qz * qw), 2.0 * (qx * qz + qy * qw)]), jnp.stack([2.0 * (qx * qy + qz * qw), 1.0 - 2.0 * (qx * qx + qz * qz), 2.0 * (qy * qz - qx * qw)]), jnp.stack([2.0 * (qx * qz - qy * qw), 2.0 * (qy * qz + qx * qw), 1.0 - 2.0 * (qx * qx + qy * qy)])])
    axis_order = jnp.array([1, 2, 0], dtype=jnp.int32)
    first_degree = jnp.take(jnp.take(rotation, axis_order, axis=0), axis_order, axis=1)
    quad_basis = jnp.array(quad_table())
    second_degree = jnp.einsum('aij,jke,bkl,ile->abe', quad_basis, rotation, quad_basis, rotation)
    assembled = jnp.zeros((9, 9, EDGES), jnp.float32)
    assembled = assembled.at[0, 0].set(1.0)
    assembled = assembled.at[1:4, 1:4].set(first_degree)
    assembled = assembled.at[4:9, 4:9].set(second_degree)
    return assembled


def set_ends(result, stream_key, least, largest):
    longest = result.shape.index(max(result.shape))
    spots = []
    for shift in (0, 1):
        where = [jax.random.randint(jax.random.fold_in(stream_key, axis), (), 0, length) for axis, length in enumerate(result.shape)]
        where[longest] = (where[longest] + shift) % result.shape[longest]
        spots.append(tuple(where))
    return result.at[spots[0]].set(least).at[spots[1]].set(largest)


def levels(own_key, extent, pieces, low, high):
    gain = 1.0
    for axis_at, shards_of in pieces:
        draws = jax.random.uniform(jax.random.fold_in(jax.random.fold_in(own_key, 6), axis_at), (shards_of,), jnp.float32, low / len(pieces), high / len(pieces))
        gain = gain * jnp.repeat(jnp.exp(draws), extent[axis_at] // shards_of).reshape((-1,) + (1,) * (len(extent) - 1 - axis_at))
    return gain


def shared_out(own_key, own, number, rows, count, top, reach, slope):
    sequence = jax.random.permutation(own_key, count)
    crowded, common = load_shares(count, rows * top, reach, slope, True), load_shares(count, rows * top, reach, slope, False)
    places = jnp.arange(count)

    def named(sizes, turn):
        used = int((sizes > 0).sum())
        fixed = max(1, used // 4)
        passed = fixed + (places - fixed + turn * (used - fixed)) % max(1, count - fixed)
        return jnp.zeros((count,), jnp.int32).at[sequence[jnp.where(places < fixed, places, passed)]].set(jnp.asarray(sizes, jnp.int32))

    sizes = jnp.where(number % 4 == 0, named(crowded, number // 4), named(common, number - number // 4 - 1))
    mixed = jax.random.permutation(jax.random.fold_in(own, 3), count)
    donor, receiver = mixed[0:count // 2 * 2:2], mixed[1:count // 2 * 2:2]
    slack = jnp.minimum(sizes[donor] - 1, reach - sizes[receiver]) // 2
    slack = jnp.where((donor == sequence[0]) | (receiver == sequence[0]) | (sizes[receiver] == 0), 0, jnp.maximum(slack, 0))
    passed = jax.random.randint(jax.random.fold_in(own, 4), (count // 2,), 0, 1 << 20) % (slack + 1)
    sizes = sizes.at[donor].add(-passed).at[receiver].add(passed)
    members = jnp.searchsorted(jnp.cumsum(sizes), jnp.arange(rows * top), side="right").astype(jnp.int32)
    grid = members.reshape(top, rows).T
    grid = grid[jax.random.permutation(jax.random.fold_in(own, 1), rows)]
    turn = jax.random.randint(jax.random.fold_in(own, 2), (rows, 1), 0, top)
    return jnp.take_along_axis(grid, (jnp.arange(top)[None, :] + turn) % top, axis=1)


def load_shares(count, total, reach, lean, full):
    loads = [(1 << 20) // math.isqrt(grade ** lean) + 1 for grade in range(1, count + 1)]
    largest = reach if full else min(reach, max(-(-total // count), total * loads[0] // sum(loads)))
    least = 1 if total - largest >= count - 1 else 0
    given, rest = [largest] + [least] * (count - 1), total - largest - least * (count - 1)
    while rest > 0:
        free = [i for i in range(1, count) if given[i] < largest] or [i for i in range(1, count) if given[i] < reach]
        whole, remaining = sum([loads[i] for i in free]), rest
        for i in free:
            extra = min(reach - given[i], max(1, remaining * loads[i] // whole), rest)
            given[i] = given[i] + extra
            rest = rest - extra
    return np.array(given)


def noise(own_key, shape, spread, limit, split=(), held_as=jnp.bfloat16):
    level = levels(own_key, shape, split, -0.22, 0.18) if split else 1.0
    result = jax.random.normal(own_key, shape, jnp.float32) * spread * level
    return jnp.minimum(jnp.maximum(result, -limit), limit).astype(held_as)


def setup_inputs(seed: int = 0) -> dict:
    keys = jax.random.split(jax.random.key(seed), 13)
    features = noise(keys[0], (ATOMS, COEF, C), 1.0, 6.0, ((0, 32),))
    cotangent = noise(keys[1], (ATOMS, COEF, C), 1.0, 6.0, ((0, 32),))
    wigner = draw_wigner(jax.random.fold_in(keys[12], 71), 0)
    pair_blocks_keys = jax.random.split(jax.random.fold_in(keys[3], 1), PAIRS // PAIRS_DEV)
    pair_blocks_turns = jax.random.permutation(jax.random.fold_in(keys[3], 3), PAIRS // PAIRS_DEV)
    pair_blocks = jax.vmap(lambda own, number: shared_out(jax.random.fold_in(keys[3], 2), own, number, PAIRS_DEV, N_ATOMS, 2, MOST, 2))(pair_blocks_keys, pair_blocks_turns).reshape((PAIRS, 2))
    pair_rows = set_ends(jax.random.randint(keys[4], (2, RPP, PAIRS), 0, BLK), jax.random.fold_in(keys[4], 1), 0, BLK - 1).astype(jnp.int32)
    edge_ends = set_ends(jax.random.randint(keys[5], (2, EDGES), 0, RPP), jax.random.fold_in(keys[5], 1), 0, RPP - 1).astype(jnp.int32)
    first_m0 = noise(keys[6], (6 * C, 4 * C), (6 * C) ** -0.5, 0.21875)
    first_m1 = noise(keys[7], (2, 4 * C, 2 * C), (8 * C) ** -0.5, 0.1875)
    first_m2 = noise(keys[8], (2, 2 * C, C), (4 * C) ** -0.5, 0.25)
    second_m0 = noise(keys[9], (3 * C, 3 * C), (3 * C) ** -0.5, 0.3125)
    second_m1 = noise(keys[10], (2, 2 * C, 2 * C), (4 * C) ** -0.5, 0.25)
    second_m2 = noise(keys[11], (2, C, C), (2 * C) ** -0.5, 0.375)
    return {"features": features, "cotangent": cotangent, "wigner": wigner, "pair_blocks": pair_blocks, "pair_rows": pair_rows, "edge_ends": edge_ends, "first_m0": first_m0, "first_m1": first_m1, "first_m2": first_m2, "second_m0": second_m0, "second_m1": second_m1, "second_m2": second_m2}


COEF_ORDER = (0, 2, 6, 3, 7, 1, 5, 8, 4)


def rotate(turned, row_block):
    return jnp.einsum("ije,ejc->eic", turned, row_block.astype(jnp.float32), precision=lax.Precision.HIGHEST)


def unrotate(turned, row_block):
    return jnp.einsum("ije,eic->ejc", turned, row_block, precision=lax.Precision.HIGHEST)


def widen_pair(pair_weights):
    upper_half = jnp.concatenate([pair_weights[0], pair_weights[1]], axis=1)
    lower_half = jnp.concatenate([-pair_weights[1], pair_weights[0]], axis=1)
    return jnp.concatenate([upper_half, lower_half], axis=0)


def narrow(gradient):
    half_rows = gradient.shape[0] // 2
    half_cols = gradient.shape[1] // 2
    return jnp.stack([gradient[:half_rows, :half_cols] + gradient[half_rows:, half_cols:],
                      gradient[:half_rows, half_cols:] - gradient[half_rows:, :half_cols]])


def forward_dot(left_rows, weight):
    return jnp.dot(left_rows, weight, preferred_element_type=jnp.float32)


def backward_dot(gradient, weight):
    return lax.dot_general(gradient, weight, (((1,), (1,)), ((), ())), preferred_element_type=jnp.float32)


def weight_dot(left_rows, gradient):
    return lax.dot_general(left_rows, gradient, (((0,), (0,)), ((), ())), preferred_element_type=jnp.float32)


def forward_part(turned, source, target, weights):
    zero_a, big_one_a, big_two_a, zero_b, big_one_b, big_two_b = weights
    row_count = source.shape[0]
    channels = source.shape[2]
    rot_source = rotate(turned, source)
    rot_target = rotate(turned, target)
    lifted = jnp.concatenate([jnp.concatenate([rot_source, rot_target], axis=2),
                              jnp.concatenate([rot_target, rot_source], axis=2)], axis=0)
    lifted = lifted.astype(jnp.bfloat16).reshape(2 * row_count, 18 * channels)
    zero_part = lifted[:, :6 * channels]
    one_part = lifted[:, 6 * channels:14 * channels]
    two_part = lifted[:, 14 * channels:]
    first_out = forward_dot(zero_part, zero_a)
    hidden = jnp.concatenate([first_out[:, :3 * channels], forward_dot(one_part, big_one_a),
                              forward_dot(two_part, big_two_a)], axis=1)
    gate_value = jax.nn.sigmoid(first_out[:, 3 * channels:])
    scalar_part = hidden[:, :channels]
    gated_part = hidden[:, channels:].reshape(2 * row_count, 8, channels)
    activated = jnp.concatenate([jax.nn.silu(scalar_part),
                                 (gated_part * gate_value[:, None, :]).reshape(2 * row_count, 8 * channels)],
                                axis=1).astype(jnp.bfloat16)
    mixed_rows = jnp.concatenate([forward_dot(activated[:, :3 * channels], zero_b),
                                  forward_dot(activated[:, 3 * channels:7 * channels], big_one_b),
                                  forward_dot(activated[:, 7 * channels:], big_two_b)], axis=1)
    mixed_rows = mixed_rows.reshape(2 * row_count, 9, channels)
    stored = (zero_part, one_part, two_part, scalar_part, gated_part, gate_value, activated)
    return unrotate(turned, mixed_rows[:row_count]), unrotate(turned, mixed_rows[row_count:]), stored


def backward_part(turned, stored, grad_target_in, grad_source_in, weights):
    zero_a, big_one_a, big_two_a, zero_b, big_one_b, big_two_b = weights
    zero_part, one_part, two_part, scalar_part, gated_part, gate_value, activated = stored
    row_count = grad_target_in.shape[0]
    channels = grad_target_in.shape[2]
    all_rows = 2 * row_count
    grad_mix = jnp.concatenate([rotate(turned, grad_target_in), rotate(turned, grad_source_in)], axis=0)
    grad_mix = grad_mix.astype(jnp.bfloat16).reshape(all_rows, 9 * channels)
    mix_zero = grad_mix[:, :3 * channels]
    mix_one = grad_mix[:, 3 * channels:7 * channels]
    mix_two = grad_mix[:, 7 * channels:]
    grad_act = jnp.concatenate([backward_dot(mix_zero, zero_b), backward_dot(mix_one, big_one_b),
                                backward_dot(mix_two, big_two_b)], axis=1)
    terms_second = (weight_dot(activated[:, :3 * channels], mix_zero),
                    narrow(weight_dot(activated[:, 3 * channels:7 * channels], mix_one)),
                    narrow(weight_dot(activated[:, 7 * channels:], mix_two)))
    head_gate = jax.nn.sigmoid(scalar_part)
    grad_scalar = grad_act[:, :channels] * head_gate * (1.0 + scalar_part * (1.0 - head_gate))
    grad_gated = grad_act[:, channels:].reshape(all_rows, 8, channels)
    gated_grad = (grad_gated * gate_value[:, None, :]).reshape(all_rows, 8 * channels)
    grad_gate = jnp.sum(grad_gated * gated_part, axis=1) * gate_value * (1.0 - gate_value)
    grad_zero = jnp.concatenate([grad_scalar, gated_grad[:, :2 * channels], grad_gate], axis=1).astype(jnp.bfloat16)
    grad_one = gated_grad[:, 2 * channels:6 * channels].astype(jnp.bfloat16)
    grad_two = gated_grad[:, 6 * channels:].astype(jnp.bfloat16)
    grad_lifted = jnp.concatenate([backward_dot(grad_zero, zero_a), backward_dot(grad_one, big_one_a),
                                   backward_dot(grad_two, big_two_a)], axis=1).reshape(all_rows, 9, 2 * channels)
    terms_first = (weight_dot(zero_part, grad_zero), narrow(weight_dot(one_part, grad_one)),
                   narrow(weight_dot(two_part, grad_two)))
    front_grad = grad_lifted[:row_count]
    back_grad = grad_lifted[row_count:]
    grad_source = unrotate(turned, front_grad[:, :, :channels] + back_grad[:, :, channels:])
    grad_target = unrotate(turned, front_grad[:, :, channels:] + back_grad[:, :, :channels])
    return grad_source, grad_target, terms_first + terms_second


def reference(features, cotangent, wigner, pair_blocks, pair_rows, edge_ends,
              first_m0, first_m1, first_m2, second_m0, second_m1, second_m2):
    channels = features.shape[2]
    coef_count = features.shape[1]
    per_device = PAIRS_DEV * EPP
    weights = (first_m0, widen_pair(first_m1), widen_pair(first_m2),
               second_m0, widen_pair(second_m1), widen_pair(second_m2))
    index_order = jnp.array(COEF_ORDER, dtype=jnp.int32)
    plain_weights = (first_m0, first_m1, first_m2, second_m0, second_m1, second_m2)

    def one_device(running, block_index):
        summed_msgs, summed_grads, totals = running
        pairs_here = lax.dynamic_slice_in_dim(pair_blocks, block_index * PAIRS_DEV, PAIRS_DEV, 0)
        rows_here = lax.dynamic_slice_in_dim(pair_rows, block_index * PAIRS_DEV, PAIRS_DEV, 2)
        ends_here = lax.dynamic_slice_in_dim(edge_ends, block_index * per_device, per_device, 1)
        turned = jnp.take(lax.dynamic_slice_in_dim(wigner, block_index * per_device, per_device, 2),
                          index_order, axis=0)
        pair_of = jnp.arange(per_device, dtype=jnp.int32) // EPP
        target = pairs_here[pair_of, 0] * BLK + rows_here[0, ends_here[0], pair_of]
        source = pairs_here[pair_of, 1] * BLK + rows_here[1, ends_here[1], pair_of]
        to_target, to_source, stored = forward_part(turned, features[source], features[target], weights)
        grad_source, grad_target, grad_terms = backward_part(turned, stored, cotangent[target],
                                                             cotangent[source], weights)
        summed_msgs = summed_msgs.at[target].add(to_target).at[source].add(to_source)
        summed_grads = summed_grads.at[source].add(grad_source).at[target].add(grad_target)
        totals = tuple(left_term + right_term for left_term, right_term in zip(totals, grad_terms))
        return (summed_msgs, summed_grads, totals), None

    initial = (jnp.zeros((BLK * N_ATOMS, coef_count, channels), jnp.float32),
               jnp.zeros((BLK * N_ATOMS, coef_count, channels), jnp.float32),
               tuple(jnp.zeros(weight.shape, jnp.float32) for weight in plain_weights))
    (summed_msgs, summed_grads, totals), unused = lax.scan(one_device, initial,
                                                           jnp.arange(N_ATOMS, dtype=jnp.int32))
    grad_scale = (2.0 * EDGES) ** -0.5
    return (summed_msgs.astype(jnp.bfloat16), summed_grads, totals[0] * grad_scale, totals[1] * grad_scale,
            totals[2] * grad_scale, totals[3] * grad_scale, totals[4] * grad_scale, totals[5] * grad_scale)
```

```python
import jax
import jax.numpy as jnp
from jax import lax
from jax.experimental import pallas as pl
from jax.experimental.pallas import tpu as pltpu
from jax.sharding import PartitionSpec as P

COEF_ORDER = (0, 2, 6, 3, 7, 1, 5, 8, 4)
DEGREES = ((0, 1), (1, 4), (4, 9))
CHUNK = 128
LANES = 128
VMEM_BYTES = 66_000_000


def degree_of(index):
    for low, high in DEGREES:
        if low <= index < high:
            return range(low, high)


def dot_nn(left, right):
    return jnp.dot(left, right, preferred_element_type=jnp.float32)


def dot_nt(left, right):
    return lax.dot_general(left, right, (((1,), (1,)), ((), ())), preferred_element_type=jnp.float32)


def dot_tn(left, right):
    return lax.dot_general(left, right, (((0,), (0,)), ((), ())), preferred_element_type=jnp.float32)


def pick_kernel(picked_ref, features_ref, cotangent_ref, out_ref):
    rows = out_ref.shape[0]
    coefs, atoms, channels = features_ref.shape
    chosen = picked_ref[...] == lax.broadcasted_iota(jnp.int32, (rows, atoms), 1)
    chosen = chosen.astype(jnp.float32).astype(jnp.bfloat16)
    for side, ref in enumerate((features_ref, cotangent_ref)):
        for j in range(coefs):
            at = (side * coefs + j) * channels
            out_ref[:, at : at + channels] = dot_nn(chosen, ref[j]).astype(jnp.bfloat16)


def owner_kernel(picked_ref, back_ref, messages_ref, grads_ref):
    rows = back_ref.shape[0]
    coefs, atoms, channels = grads_ref.shape
    chosen = picked_ref[...] == lax.broadcasted_iota(jnp.int32, (rows, atoms), 1)
    chosen = chosen.astype(jnp.float32).astype(jnp.bfloat16)
    for j in range(coefs):
        at = j * channels
        messages_ref[j] = dot_tn(chosen, back_ref[:, at : at + channels]).astype(jnp.bfloat16)
        at = (coefs + j) * channels
        grads_ref[j] = dot_tn(chosen, back_ref[:, at : at + channels])


def spread_kernel(packed_ref, *out_refs):
    at = 0
    for ref in out_refs:
        views = [ref] if len(ref.shape) == 2 else [ref.at[0], ref.at[1]]
        for view in views:
            height, width = view.shape
            for col in range(0, width, LANES):
                view[:, col : col + LANES] = packed_ref[at : at + height, :].astype(jnp.float32)
                at += height


def widen_into(ref, pair_ref):
    rows, cols = pair_ref.shape[1], pair_ref.shape[2]
    ref[:rows, :cols] = pair_ref[0]
    ref[:rows, cols:] = pair_ref[1]
    ref[rows:, :cols] = (-pair_ref[1].astype(jnp.float32)).astype(jnp.bfloat16)
    ref[rows:, cols:] = pair_ref[0]


def edge_kernel(
    flat_ref, wig_ref, pos_ref, fa0, fa1, fa2, sb0, sb1, sb2,
    slots_ref, packed_ref,
    acc, wa1, wa2, wb1, wb2, ga0, ga1, ga2, gb0, gb1, gb2,
    got, z, hid, gate_ref, act, mixed, dmix, dout, dz, contrib,
):
    C = LANES
    n_slots = flat_ref.shape[0]
    edges = wig_ref.shape[0]
    half = 9 * C
    widen_into(wa1, fa1)
    widen_into(wa2, fa2)
    widen_into(wb1, sb1)
    widen_into(wb2, sb2)
    for ref in (acc, ga0, ga1, ga2, gb0, gb1, gb2):
        ref[...] = jnp.zeros_like(ref)

    def step(index, carry):
        base = pl.multiple_of(index * CHUNK, CHUNK)
        span = pl.ds(base, CHUNK)
        slot_ids = lax.broadcasted_iota(jnp.int32, (CHUNK, n_slots), 1)

        def one_hot(which):
            hit = pos_ref[span, which : which + 1] == slot_ids
            return hit.astype(jnp.float32).astype(jnp.bfloat16)

        hot = jnp.concatenate([one_hot(0), one_hot(1)], axis=0)
        for c in range(0, 2 * half, 256):
            got[:, c : c + 256] = dot_nn(hot, flat_ref[:, c : c + 256])
        T, S = slice(0, CHUNK), slice(CHUNK, 2 * CHUNK)
        wig = wig_ref[span, :]

        def entry(row, col):
            k = row * 9 + col
            return jnp.broadcast_to(wig[:, k : k + 1], (CHUNK, C))

        for i, o in enumerate(COEF_ORDER):
            sums = [None] * 4
            for j in degree_of(o):
                w = entry(o, j)
                parts = (
                    got[T, j * C : (j + 1) * C],
                    got[S, j * C : (j + 1) * C],
                    got[T, half + j * C : half + (j + 1) * C],
                    got[S, half + j * C : half + (j + 1) * C],
                )
                sums = [w * p if s is None else s + w * p for s, p in zip(sums, parts)]
            rt, rs, ct, cs = (s.astype(jnp.bfloat16) for s in sums)
            left = slice(2 * i * C, (2 * i + 1) * C)
            right = slice((2 * i + 1) * C, (2 * i + 2) * C)
            z[T, left] = rs
            z[T, right] = rt
            z[S, left] = rt
            z[S, right] = rs
            dmix[T, i * C : (i + 1) * C] = ct
            dmix[S, i * C : (i + 1) * C] = cs

        first = dot_nn(z[:, : 6 * C], fa0[...])
        hid[:, : 3 * C] = first[:, : 3 * C]
        gate_ref[...] = jax.nn.sigmoid(first[:, 3 * C :])
        hid[:, 3 * C : 7 * C] = dot_nn(z[:, 6 * C : 14 * C], wa1[...])
        hid[:, 7 * C :] = dot_nn(z[:, 14 * C :], wa2[...])
        gate = gate_ref[...]
        h0 = hid[:, :C]
        act[:, :C] = (h0 * jax.nn.sigmoid(h0)).astype(jnp.bfloat16)
        for k in range(1, 9):
            act[:, k * C : (k + 1) * C] = (hid[:, k * C : (k + 1) * C] * gate).astype(jnp.bfloat16)
        mixed[:, : 3 * C] = dot_nn(act[:, : 3 * C], sb0[...])
        mixed[:, 3 * C : 7 * C] = dot_nn(act[:, 3 * C : 7 * C], wb1[...])
        mixed[:, 7 * C :] = dot_nn(act[:, 7 * C :], wb2[...])

        gb0[...] += dot_tn(act[:, : 3 * C], dmix[:, : 3 * C])
        gb1[...] += dot_tn(act[:, 3 * C : 7 * C], dmix[:, 3 * C : 7 * C])
        gb2[...] += dot_tn(act[:, 7 * C :], dmix[:, 7 * C :])
        dact = dz
        dact[:, : 3 * C] = dot_nt(dmix[:, : 3 * C], sb0[...])
        dact[:, 3 * C : 7 * C] = dot_nt(dmix[:, 3 * C : 7 * C], wb1[...])
        dact[:, 7 * C : 9 * C] = dot_nt(dmix[:, 7 * C :], wb2[...])
        head = jax.nn.sigmoid(h0)
        dout[:, :C] = (dact[:, :C] * head * (1.0 + h0 * (1.0 - head))).astype(jnp.bfloat16)
        grad_gate = None
        for k in range(1, 9):
            d = dact[:, k * C : (k + 1) * C]
            term = d * hid[:, k * C : (k + 1) * C]
            grad_gate = term if grad_gate is None else grad_gate + term
            at = k * C if k < 3 else (k + 1) * C
            dout[:, at : at + C] = (d * gate).astype(jnp.bfloat16)
        dout[:, 3 * C : 4 * C] = (grad_gate * gate * (1.0 - gate)).astype(jnp.bfloat16)

        ga0[...] += dot_tn(z[:, : 6 * C], dout[:, : 4 * C])
        ga1[...] += dot_tn(z[:, 6 * C : 14 * C], dout[:, 4 * C : 8 * C])
        ga2[...] += dot_tn(z[:, 14 * C :], dout[:, 8 * C :])
        dz[:, : 6 * C] = dot_nt(dout[:, : 4 * C], fa0[...])
        dz[:, 6 * C : 14 * C] = dot_nt(dout[:, 4 * C : 8 * C], wa1[...])
        dz[:, 14 * C :] = dot_nt(dout[:, 8 * C :], wa2[...])

        for j in range(9):
            sums = [None] * 4
            for i, o in enumerate(COEF_ORDER):
                if o not in degree_of(j):
                    continue
                w = entry(o, j)
                left = slice(2 * i * C, (2 * i + 1) * C)
                right = slice((2 * i + 1) * C, (2 * i + 2) * C)
                parts = (
                    mixed[T, i * C : (i + 1) * C],
                    mixed[S, i * C : (i + 1) * C],
                    dz[T, right] + dz[S, left],
                    dz[T, left] + dz[S, right],
                )
                sums = [w * p if s is None else s + w * p for s, p in zip(sums, parts)]
            for row, col, value in (
                (0, j * C, sums[0]),
                (CHUNK, j * C, sums[1]),
                (0, half + j * C, sums[2]),
                (CHUNK, half + j * C, sums[3]),
            ):
                upper = value.astype(jnp.bfloat16)
                contrib[row : row + CHUNK, col : col + C] = upper
                contrib[2 * CHUNK + row : 3 * CHUNK + row, col : col + C] = (
                    value - upper.astype(jnp.float32)
                ).astype(jnp.bfloat16)
        hot_twice = jnp.concatenate([hot, hot], axis=0)
        for c in range(0, 2 * half, 256):
            acc[:, c : c + 256] += dot_tn(hot_twice, contrib[:, c : c + 256])
        return carry

    lax.fori_loop(0, edges // CHUNK, step, 0)
    slots_ref[...] = acc[...].astype(jnp.bfloat16)

    at = 0

    def put(value):
        nonlocal at
        height = value.shape[0]
        for col in range(0, value.shape[1], C):
            packed_ref[at : at + height, :] = value[:, col : col + C].astype(jnp.bfloat16)
            at += height

    def put_pair(ref):
        rows, cols = ref.shape[0] // 2, ref.shape[1] // 2
        put(ref[:rows, :cols] + ref[rows:, cols:])
        put(ref[:rows, cols:] - ref[rows:, :cols])

    put(ga0[...])
    put_pair(ga1)
    put_pair(ga2)
    put(gb0[...])
    put_pair(gb1)
    put_pair(gb2)
    rest = packed_ref.shape[0] - at
    if rest:
        packed_ref[at:, :] = jnp.zeros((rest, C), jnp.bfloat16)


def call(kernel, out_shape, scratch=(), flops=1_000_000):
    many = isinstance(out_shape, (tuple, list))
    whole = pl.BlockSpec(memory_space=pltpu.VMEM)

    def run(*operands):
        return pl.pallas_call(
            kernel,
            out_shape=out_shape,
            in_specs=[whole] * len(operands),
            out_specs=[whole] * len(out_shape) if many else whole,
            scratch_shapes=list(scratch),
            compiler_params=pltpu.CompilerParams(vmem_limit_bytes=VMEM_BYTES),
            cost_estimate=pl.CostEstimate(flops=flops, bytes_accessed=4_000_000, transcendentals=0),
        )(*operands)

    return run


def exchange(value):
    return lax.all_to_all(value, "atoms", split_axis=0, concat_axis=0, tiled=True)


def local(features, cotangent, wigner, pair_blocks, pair_rows, edge_ends, *weights):
    peers = lax.axis_size("atoms")
    atoms, coefs, channels = features.shape
    pair_count = pair_blocks.shape[0]
    row_width = pair_rows.shape[1]
    edges = edge_ends.shape[1]
    per_pair = edges // pair_count
    slot_count = max(2, 4 * pair_count // peers)
    width = slot_count * row_width
    padded = -(-width // 16) * 16
    both = 2 * coefs * channels
    f32, bf16 = jnp.float32, jnp.bfloat16

    owners = pair_blocks.reshape(2 * pair_count)
    spots = jnp.arange(2 * pair_count, dtype=jnp.int32)
    rank = jnp.sum(
        (owners[:, None] == owners[None, :]) & (spots[:, None] > spots[None, :]), axis=1
    ).astype(jnp.int32)
    end_rows = jnp.transpose(pair_rows, (2, 0, 1)).reshape(2 * pair_count, row_width)
    place = owners * slot_count + rank
    names = jnp.arange(peers * slot_count, dtype=jnp.int32)
    request = jnp.sum(
        jnp.where((place[None, :] == names[:, None])[:, :, None], end_rows[None], 0), axis=1
    ).astype(jnp.int32)
    requested = exchange(request.reshape(peers, width))
    picked = jnp.pad(requested, ((0, 0), (0, padded - width)), constant_values=-1)
    picked = picked.reshape(peers * padded, 1)

    n_slots = peers * padded
    chosen = call(pick_kernel, jax.ShapeDtypeStruct((n_slots, both), bf16))(
        picked, jnp.transpose(features, (1, 0, 2)), jnp.transpose(cotangent, (1, 0, 2))
    )
    flat = exchange(chosen.reshape(peers, padded, both)).reshape(n_slots, both)

    end_slot = (owners * padded + rank * row_width).reshape(pair_count, 1, 2)
    ends = jnp.broadcast_to(end_slot, (pair_count, per_pair, 2)).reshape(edges, 2)
    positions = ends + jnp.transpose(edge_ends)
    wig = jnp.transpose(wigner.reshape(coefs * coefs, edges))

    total_rows = sum(w.size for w in weights) // LANES
    share = -(-total_rows // (16 * peers)) * 16
    rows = 2 * CHUNK
    V = pltpu.VMEM
    first_m0, first_m1, first_m2, second_m0, second_m1, second_m2 = weights
    wide = [(2 * w.shape[1], 2 * w.shape[2]) for w in (first_m1, first_m2, second_m1, second_m2)]
    scratch = [
        V((n_slots, both), f32),
        *[V(shape, bf16) for shape in wide],
        V(first_m0.shape, f32), V(wide[0], f32), V(wide[1], f32),
        V(second_m0.shape, f32), V(wide[2], f32), V(wide[3], f32),
        V((rows, both), f32),
        V((rows, both), bf16),
        V((rows, coefs * channels), f32),
        V((rows, channels), f32),
        V((rows, coefs * channels), bf16),
        V((rows, coefs * channels), f32),
        V((rows, coefs * channels), bf16),
        V((rows, (coefs + 1) * channels), bf16),
        V((rows, both), f32),
        V((2 * rows, both), bf16),
    ]
    slots, packed = call(
        edge_kernel,
        [
            jax.ShapeDtypeStruct((n_slots, both), bf16),
            jax.ShapeDtypeStruct((peers * share, LANES), bf16),
        ],
        scratch,
        flops=10_000_000_000,
    )(flat, wig, positions, *weights)

    grad_scale = (2.0 * edges * peers) ** (-0.5)
    parts = exchange(packed.reshape(peers, share, LANES))
    back = exchange(slots.reshape(peers, padded, both)).reshape(n_slots, both)
    mine = (jnp.sum(parts.astype(f32), axis=0) * grad_scale).astype(bf16)
    everyone = exchange(jnp.broadcast_to(mine[None], (peers, share, LANES)))
    messages, grads = call(
        owner_kernel,
        [
            jax.ShapeDtypeStruct((coefs, atoms, channels), bf16),
            jax.ShapeDtypeStruct((coefs, atoms, channels), f32),
        ],
    )(picked, back)
    outs = call(spread_kernel, [jax.ShapeDtypeStruct(w.shape, f32) for w in weights])(
        everyone.reshape(peers * share, LANES)
    )
    return (jnp.transpose(messages, (1, 0, 2)), jnp.transpose(grads, (1, 0, 2)), *outs)


def solution(mesh):
    in_specs = (
        P("atoms", None, None),
        P("atoms", None, None),
        P(None, None, "atoms"),
        P("atoms", None),
        P(None, None, "atoms"),
        P(None, "atoms"),
        P(),
        P(),
        P(),
        P(),
        P(),
        P(),
    )
    out_specs = (P("atoms", None, None), P("atoms", None, None), P(), P(), P(), P(), P(), P())
    return jax.shard_map(local, mesh=mesh, in_specs=in_specs, out_specs=out_specs, check_vma=False)
```

```python
import jax
import jax.numpy as jnp
from jax import lax
from jax.experimental import pallas as pl
from jax.experimental.pallas import tpu as pltpu
from jax.sharding import PartitionSpec as P

COEF_ORDER = (0, 2, 6, 3, 7, 1, 5, 8, 4)
DEGREES = ((0, 1), (1, 4), (4, 9))
CHUNK = 128
LANES = 128
VMEM_BYTES = 66_000_000


def degree_of(index):
    for low, high in DEGREES:
        if low <= index < high:
            return range(low, high)


def dot_nn(left, right):
    return jnp.dot(left, right, preferred_element_type=jnp.float32)


def dot_nt(left, right):
    return lax.dot_general(left, right, (((1,), (1,)), ((), ())), preferred_element_type=jnp.float32)


def dot_tn(left, right):
    return lax.dot_general(left, right, (((0,), (0,)), ((), ())), preferred_element_type=jnp.float32)


def pick_kernel(picked_ref, features_ref, cotangent_ref, out_ref):
    rows = out_ref.shape[0]
    coefs, atoms, channels = features_ref.shape
    chosen = picked_ref[...] == lax.broadcasted_iota(jnp.int32, (rows, atoms), 1)
    chosen = chosen.astype(jnp.float32).astype(jnp.bfloat16)
    for side, ref in enumerate((features_ref, cotangent_ref)):
        for j in range(coefs):
            at = (side * coefs + j) * channels
            out_ref[:, at : at + channels] = dot_nn(chosen, ref[j]).astype(jnp.bfloat16)


def owner_kernel(picked_ref, back_ref, messages_ref, grads_ref):
    rows = back_ref.shape[0]
    coefs, atoms, channels = grads_ref.shape
    chosen = picked_ref[...] == lax.broadcasted_iota(jnp.int32, (rows, atoms), 1)
    chosen = chosen.astype(jnp.float32).astype(jnp.bfloat16)
    for j in range(coefs):
        at = j * channels
        messages_ref[j] = dot_tn(chosen, back_ref[:, at : at + channels]).astype(jnp.bfloat16)
        at = (coefs + j) * channels
        grads_ref[j] = dot_tn(chosen, back_ref[:, at : at + channels])


def spread_kernel(packed_ref, *out_refs):
    at = 0
    for ref in out_refs:
        views = [ref] if len(ref.shape) == 2 else [ref.at[0], ref.at[1]]
        for view in views:
            height, width = view.shape
            for col in range(0, width, LANES):
                view[:, col : col + LANES] = packed_ref[at : at + height, :].astype(jnp.float32)
                at += height


def widen_into(ref, pair_ref):
    rows, cols = pair_ref.shape[1], pair_ref.shape[2]
    ref[:rows, :cols] = pair_ref[0]
    ref[:rows, cols:] = pair_ref[1]
    ref[rows:, :cols] = (-pair_ref[1].astype(jnp.float32)).astype(jnp.bfloat16)
    ref[rows:, cols:] = pair_ref[0]


def edge_kernel(
    flat_ref, wig_ref, pos_ref, fa0, fa1, fa2, sb0, sb1, sb2,
    slots_ref, packed_ref,
    acc, wa1, wa2, wb1, wb2, ga0, ga1, ga2, gb0, gb1, gb2,
    got, z, hid, gate_ref, act, mixed, dmix, dout, dz, contrib,
):
    C = LANES
    n_slots = flat_ref.shape[0]
    edges = wig_ref.shape[0]
    half = 9 * C
    widen_into(wa1, fa1)
    widen_into(wa2, fa2)
    widen_into(wb1, sb1)
    widen_into(wb2, sb2)
    for ref in (acc, ga0, ga1, ga2, gb0, gb1, gb2):
        ref[...] = jnp.zeros_like(ref)

    def step(index, carry):
        base = pl.multiple_of(index * CHUNK, CHUNK)
        span = pl.ds(base, CHUNK)
        slot_ids = lax.broadcasted_iota(jnp.int32, (CHUNK, n_slots), 1)

        def one_hot(which):
            hit = pos_ref[span, which : which + 1] == slot_ids
            return hit.astype(jnp.float32).astype(jnp.bfloat16)

        hot = jnp.concatenate([one_hot(0), one_hot(1)], axis=0)
        for c in range(0, 2 * half, 256):
            got[:, c : c + 256] = dot_nn(hot, flat_ref[:, c : c + 256])
        T, S = slice(0, CHUNK), slice(CHUNK, 2 * CHUNK)
        wig = wig_ref[span, :]

        def entry(row, col):
            k = row * 9 + col
            return jnp.broadcast_to(wig[:, k : k + 1], (CHUNK, C))

        for i, o in enumerate(COEF_ORDER):
            sums = [None] * 4
            for j in degree_of(o):
                w = entry(o, j)
                parts = (
                    got[T, j * C : (j + 1) * C],
                    got[S, j * C : (j + 1) * C],
                    got[T, half + j * C : half + (j + 1) * C],
                    got[S, half + j * C : half + (j + 1) * C],
                )
                sums = [w * p if s is None else s + w * p for s, p in zip(sums, parts)]
            rt, rs, ct, cs = (s.astype(jnp.bfloat16) for s in sums)
            left = slice(2 * i * C, (2 * i + 1) * C)
            right = slice((2 * i + 1) * C, (2 * i + 2) * C)
            z[T, left] = rs
            z[T, right] = rt
            z[S, left] = rt
            z[S, right] = rs
            dmix[T, i * C : (i + 1) * C] = ct
            dmix[S, i * C : (i + 1) * C] = cs

        first = dot_nn(z[:, : 6 * C], fa0[...])
        hid[:, : 3 * C] = first[:, : 3 * C]
        gate_ref[...] = jax.nn.sigmoid(first[:, 3 * C :])
        hid[:, 3 * C : 7 * C] = dot_nn(z[:, 6 * C : 14 * C], wa1[...])
        hid[:, 7 * C :] = dot_nn(z[:, 14 * C :], wa2[...])
        gate = gate_ref[...]
        h0 = hid[:, :C]
        act[:, :C] = (h0 * jax.nn.sigmoid(h0)).astype(jnp.bfloat16)
        for k in range(1, 9):
            act[:, k * C : (k + 1) * C] = (hid[:, k * C : (k + 1) * C] * gate).astype(jnp.bfloat16)
        mixed[:, : 3 * C] = dot_nn(act[:, : 3 * C], sb0[...])
        mixed[:, 3 * C : 7 * C] = dot_nn(act[:, 3 * C : 7 * C], wb1[...])
        mixed[:, 7 * C :] = dot_nn(act[:, 7 * C :], wb2[...])

        gb0[...] += dot_tn(act[:, : 3 * C], dmix[:, : 3 * C])
        gb1[...] += dot_tn(act[:, 3 * C : 7 * C], dmix[:, 3 * C : 7 * C])
        gb2[...] += dot_tn(act[:, 7 * C :], dmix[:, 7 * C :])
        dact = dz
        dact[:, : 3 * C] = dot_nt(dmix[:, : 3 * C], sb0[...])
        dact[:, 3 * C : 7 * C] = dot_nt(dmix[:, 3 * C : 7 * C], wb1[...])
        dact[:, 7 * C : 9 * C] = dot_nt(dmix[:, 7 * C :], wb2[...])
        head = jax.nn.sigmoid(h0)
        dout[:, :C] = (dact[:, :C] * head * (1.0 + h0 * (1.0 - head))).astype(jnp.bfloat16)
        grad_gate = None
        for k in range(1, 9):
            d = dact[:, k * C : (k + 1) * C]
            term = d * hid[:, k * C : (k + 1) * C]
            grad_gate = term if grad_gate is None else grad_gate + term
            at = k * C if k < 3 else (k + 1) * C
            dout[:, at : at + C] = (d * gate).astype(jnp.bfloat16)
        dout[:, 3 * C : 4 * C] = (grad_gate * gate * (1.0 - gate)).astype(jnp.bfloat16)

        ga0[...] += dot_tn(z[:, : 6 * C], dout[:, : 4 * C])
        ga1[...] += dot_tn(z[:, 6 * C : 14 * C], dout[:, 4 * C : 8 * C])
        ga2[...] += dot_tn(z[:, 14 * C :], dout[:, 8 * C :])
        dz[:, : 6 * C] = dot_nt(dout[:, : 4 * C], fa0[...])
        dz[:, 6 * C : 14 * C] = dot_nt(dout[:, 4 * C : 8 * C], wa1[...])
        dz[:, 14 * C :] = dot_nt(dout[:, 8 * C :], wa2[...])

        for j in range(9):
            sums = [None] * 4
            for i, o in enumerate(COEF_ORDER):
                if o not in degree_of(j):
                    continue
                w = entry(o, j)
                left = slice(2 * i * C, (2 * i + 1) * C)
                right = slice((2 * i + 1) * C, (2 * i + 2) * C)
                parts = (
                    mixed[T, i * C : (i + 1) * C],
                    mixed[S, i * C : (i + 1) * C],
                    dz[T, right] + dz[S, left],
                    dz[T, left] + dz[S, right],
                )
                sums = [w * p if s is None else s + w * p for s, p in zip(sums, parts)]
            for row, col, value in (
                (0, j * C, sums[0]),
                (CHUNK, j * C, sums[1]),
                (0, half + j * C, sums[2]),
                (CHUNK, half + j * C, sums[3]),
            ):
                upper = value.astype(jnp.bfloat16)
                contrib[row : row + CHUNK, col : col + C] = upper
                contrib[2 * CHUNK + row : 3 * CHUNK + row, col : col + C] = (
                    value - upper.astype(jnp.float32)
                ).astype(jnp.bfloat16)
        hot_twice = jnp.concatenate([hot, hot], axis=0)
        for c in range(0, 2 * half, 256):
            acc[:, c : c + 256] += dot_tn(hot_twice, contrib[:, c : c + 256])
        return carry

    lax.fori_loop(0, edges // CHUNK, step, 0)
    slots_ref[...] = acc[...].astype(jnp.bfloat16)

    at = 0

    def put(value):
        nonlocal at
        height = value.shape[0]
        for col in range(0, value.shape[1], C):
            packed_ref[at : at + height, :] = value[:, col : col + C].astype(jnp.bfloat16)
            at += height

    def put_pair(ref):
        rows, cols = ref.shape[0] // 2, ref.shape[1] // 2
        put(ref[:rows, :cols] + ref[rows:, cols:])
        put(ref[:rows, cols:] - ref[rows:, :cols])

    put(ga0[...])
    put_pair(ga1)
    put_pair(ga2)
    put(gb0[...])
    put_pair(gb1)
    put_pair(gb2)
    rest = packed_ref.shape[0] - at
    if rest:
        packed_ref[at:, :] = jnp.zeros((rest, C), jnp.bfloat16)


def call(kernel, out_shape, scratch=(), flops=1_000_000):
    many = isinstance(out_shape, (tuple, list))
    whole = pl.BlockSpec(memory_space=pltpu.VMEM)

    def run(*operands):
        return pl.pallas_call(
            kernel,
            out_shape=out_shape,
            in_specs=[whole] * len(operands),
            out_specs=[whole] * len(out_shape) if many else whole,
            scratch_shapes=list(scratch),
            compiler_params=pltpu.CompilerParams(vmem_limit_bytes=VMEM_BYTES),
            cost_estimate=pl.CostEstimate(flops=flops, bytes_accessed=4_000_000, transcendentals=0),
        )(*operands)

    return run


def exchange(value):
    return lax.all_to_all(value, "atoms", split_axis=0, concat_axis=0, tiled=True)


def grouped(value, groups):
    return lax.all_to_all(
        value, "atoms", split_axis=0, concat_axis=0, tiled=True, axis_index_groups=groups
    )


def local(features, cotangent, wigner, pair_blocks, pair_rows, edge_ends, *weights):
    peers = lax.axis_size("atoms")
    atoms, coefs, channels = features.shape
    pair_count = pair_blocks.shape[0]
    row_width = pair_rows.shape[1]
    edges = edge_ends.shape[1]
    per_pair = edges // pair_count
    slot_count = max(2, 4 * pair_count // peers)
    width = slot_count * row_width
    padded = -(-width // 16) * 16
    both = 2 * coefs * channels
    f32, bf16 = jnp.float32, jnp.bfloat16

    owners = pair_blocks.reshape(2 * pair_count)
    spots = jnp.arange(2 * pair_count, dtype=jnp.int32)
    rank = jnp.sum(
        (owners[:, None] == owners[None, :]) & (spots[:, None] > spots[None, :]), axis=1
    ).astype(jnp.int32)
    end_rows = jnp.transpose(pair_rows, (2, 0, 1)).reshape(2 * pair_count, row_width)
    place = owners * slot_count + rank
    names = jnp.arange(peers * slot_count, dtype=jnp.int32)
    request = jnp.sum(
        jnp.where((place[None, :] == names[:, None])[:, :, None], end_rows[None], 0), axis=1
    ).astype(jnp.int32)
    requested = exchange(request.reshape(peers, width))
    picked = jnp.pad(requested, ((0, 0), (0, padded - width)), constant_values=-1)
    picked = picked.reshape(peers * padded, 1)

    n_slots = peers * padded
    chosen = call(pick_kernel, jax.ShapeDtypeStruct((n_slots, both), bf16))(
        picked, jnp.transpose(features, (1, 0, 2)), jnp.transpose(cotangent, (1, 0, 2))
    )
    flat = exchange(chosen.reshape(peers, padded, both)).reshape(n_slots, both)

    end_slot = (owners * padded + rank * row_width).reshape(pair_count, 1, 2)
    ends = jnp.broadcast_to(end_slot, (pair_count, per_pair, 2)).reshape(edges, 2)
    positions = ends + jnp.transpose(edge_ends)
    wig = jnp.transpose(wigner.reshape(coefs * coefs, edges))

    total_rows = sum(w.size for w in weights) // LANES
    share = -(-total_rows // (16 * peers)) * 16
    rows = 2 * CHUNK
    V = pltpu.VMEM
    first_m0, first_m1, first_m2, second_m0, second_m1, second_m2 = weights
    wide = [(2 * w.shape[1], 2 * w.shape[2]) for w in (first_m1, first_m2, second_m1, second_m2)]
    scratch = [
        V((n_slots, both), f32),
        *[V(shape, bf16) for shape in wide],
        V(first_m0.shape, f32), V(wide[0], f32), V(wide[1], f32),
        V(second_m0.shape, f32), V(wide[2], f32), V(wide[3], f32),
        V((rows, both), f32),
        V((rows, both), bf16),
        V((rows, coefs * channels), f32),
        V((rows, channels), f32),
        V((rows, coefs * channels), bf16),
        V((rows, coefs * channels), f32),
        V((rows, coefs * channels), bf16),
        V((rows, (coefs + 1) * channels), bf16),
        V((rows, both), f32),
        V((2 * rows, both), bf16),
    ]
    slots, packed = call(
        edge_kernel,
        [
            jax.ShapeDtypeStruct((n_slots, both), bf16),
            jax.ShapeDtypeStruct((peers * share, LANES), bf16),
        ],
        scratch,
        flops=10_000_000_000,
    )(flat, wig, positions, *weights)

    grad_scale = (2.0 * edges * peers) ** (-0.5)
    back = exchange(slots.reshape(peers, padded, both)).reshape(n_slots, both)
    near_count = 8 if peers % 8 == 0 else 1
    far_count = peers // near_count
    near = [[h * near_count + n for n in range(near_count)] for h in range(far_count)]
    far = [[h * near_count + n for h in range(far_count)] for n in range(near_count)]
    parts = grouped(packed.reshape(near_count, far_count * share, LANES), near)
    block = jnp.sum(parts.astype(f32), axis=0).astype(bf16)
    parts = grouped(block.reshape(far_count, share, LANES), far)
    mine = (jnp.sum(parts.astype(f32), axis=0) * grad_scale).astype(bf16)
    block = grouped(jnp.broadcast_to(mine[None], (far_count, share, LANES)), far)
    block = block.reshape(1, far_count * share, LANES)
    everyone = grouped(jnp.broadcast_to(block, (near_count, far_count * share, LANES)), near)
    messages, grads = call(
        owner_kernel,
        [
            jax.ShapeDtypeStruct((coefs, atoms, channels), bf16),
            jax.ShapeDtypeStruct((coefs, atoms, channels), f32),
        ],
    )(picked, back)
    outs = call(spread_kernel, [jax.ShapeDtypeStruct(w.shape, f32) for w in weights])(
        everyone.reshape(peers * share, LANES)
    )
    return (jnp.transpose(messages, (1, 0, 2)), jnp.transpose(grads, (1, 0, 2)), *outs)


def solution(mesh):
    in_specs = (
        P("atoms", None, None),
        P("atoms", None, None),
        P(None, None, "atoms"),
        P("atoms", None),
        P(None, None, "atoms"),
        P(None, "atoms"),
        P(),
        P(),
        P(),
        P(),
        P(),
        P(),
    )
    out_specs = (P("atoms", None, None), P("atoms", None, None), P(), P(), P(), P(), P(), P())
    return jax.shard_map(local, mesh=mesh, in_specs=in_specs, out_specs=out_specs, check_vma=False)
```
